512 devices in a mesh: expert: 8 (over z_hi, x), shard: 64 (over y, z_lo, core).
Axes of the slice: x: 4, y: 4, z: 16 (z_hi: 2, z_lo: 8; z = z_hi * 8 + z_lo), core: 2. Of those that a mesh axis runs over, the one named last changes fastest.
Arguments:
- tokens: bfloat16 [1024, 2048], P('expert', 'shard'), may hold values from -6 to 6
- cotangent: bfloat16 [1024, 2048], P('expert', 'shard'), may hold values from -6 to 6
- expert_ids: int32 [1024, 2], P('expert'), may hold values from 0 to 7, all different within a row; in each aligned block of 128 rows (0 to 127, 128 to 255, ...) at most 48 rows name the same one
- route_weights: float32 [1024, 2], P('expert'), may hold values from 0.2 to 1
- dense_gate: bfloat16 [2048, 11008], P('expert', 'shard'), may hold values from -0.125 to 0.125
- dense_up: bfloat16 [2048, 11008], P('expert', 'shard'), may hold values from -0.125 to 0.125
- dense_down: bfloat16 [11008, 2048], P('shard', 'expert'), may hold values from -0.15625 to 0.15625
- noise_gate: bfloat16 [8, 2048, 1280], P('expert', None, 'shard'), may hold values from -0.125 to 0.125
- noise_up: bfloat16 [8, 2048, 1280], P('expert', None, 'shard'), may hold values from -0.125 to 0.125
- noise_down: bfloat16 [8, 1280, 2048], P('expert', 'shard'), may hold values from -0.0546875 to 0.0546875
Outputs:
- mixed: bfloat16 [1024, 2048], P('expert', 'shard')
- grad_gate: bfloat16 [8, 12288, 2048], P('expert', 'shard')
- grad_up: bfloat16 [8, 12288, 2048], P('expert', 'shard')
- grad_down: bfloat16 [8, 12288, 2048], P('expert', 'shard')
The draws below stay inside these ranges and needn't reach their ends.
Inputs may be any that keep to these rules, and one draw needn't show every extreme that they name: `expert_ids`: the two experts of a token differ. Within each aligned block of 128 tokens no expert is named by more than 48 tokens, a bound that some block reaches.
All inputs are finite; a program needn't handle non-finite values.
Results may differ from the reference program's by a relative error of at most 0.0058.
Values may be sent and summed in bfloat16 or wider, within the bound.
No kernel may reach another device: no remote copies, remote signals or barrier semaphores. Data moves between devices by JAX's collectives and lax.ppermute only.
A program may use at most 64 MiB of HBM per device.

```python
import math
import jax
import jax.numpy as jnp
import numpy as np

D = 2048
FF = 11008
FFW = 12288
TOK_DEV = 128
TOP = 2
EXPERTS = 8
TOKENS = 1024
CAP = 48
N_SHARD = 64


def with_spikes(drawn, key, source, target, parts, factor):
    owner, partner = [(jnp.arange(drawn.shape[position]) // (drawn.shape[position] // parts)).reshape([-1 if axis == position else 1 for axis in range(drawn.ndim)]) for position in (source, target)]
    chosen = jax.random.permutation(key, parts)[partner]
    strong = (owner == chosen) | (owner == (partner + parts // 2) % parts)
    return jnp.where(strong, factor * drawn, drawn)


def block_levels(rng, extent, pieces, smallest, top_value):
    factor_of = 1.0
    for axis_at, parts in pieces:
        draws = jax.random.uniform(jax.random.fold_in(jax.random.fold_in(rng, 6), axis_at), (parts,), jnp.float32, smallest / len(pieces), top_value / len(pieces))
        factor_of = factor_of * jnp.repeat(jnp.exp(draws), extent[axis_at] // parts).reshape((-1,) + (1,) * (len(extent) - 1 - axis_at))
    return factor_of


def assign_block(key, own, number, rows, number_of, top, bound, lean):
    order = jax.random.permutation(key, number_of)
    heavy_load, common = portions_of(number_of, rows * top, bound, lean, True), portions_of(number_of, rows * top, bound, lean, False)
    places = jnp.arange(number_of)

    def named(tallies, offset_by):
        used = int((tallies > 0).sum())
        fixed = max(1, used // 4)
        moved = fixed + (places - fixed + offset_by * (used - fixed)) % max(1, number_of - fixed)
        return jnp.zeros((number_of,), jnp.int32).at[order[jnp.where(places < fixed, places, moved)]].set(jnp.asarray(tallies, jnp.int32))

    tallies = jnp.where(number % 4 == 0, named(heavy_load, number // 4), named(common, number - number // 4 - 1))
    mixed = jax.random.permutation(jax.random.fold_in(own, 3), number_of)
    giver, taker = mixed[0:number_of // 2 * 2:2], mixed[1:number_of // 2 * 2:2]
    room = jnp.minimum(tallies[giver] - 1, bound - tallies[taker]) // 2
    room = jnp.where((giver == order[0]) | (taker == order[0]) | (tallies[taker] == 0), 0, jnp.maximum(room, 0))
    moved = jax.random.randint(jax.random.fold_in(own, 4), (number_of // 2,), 0, 1 << 20) % (room + 1)
    tallies = tallies.at[giver].add(-moved).at[taker].add(moved)
    labels = jnp.searchsorted(jnp.cumsum(tallies), jnp.arange(rows * top), side="right").astype(jnp.int32)
    table = labels.reshape(top, rows).T
    table = table[jax.random.permutation(jax.random.fold_in(own, 1), rows)]
    offset_by = jax.random.randint(jax.random.fold_in(own, 2), (rows, 1), 0, top)
    return jnp.take_along_axis(table, (jnp.arange(top)[None, :] + offset_by) % top, axis=1)


def portions_of(amount, total, bound, lean, full):
    loads = [(1 << 20) // math.isqrt(grade ** lean) + 1 for grade in range(1, amount + 1)]
    largest = bound if full else min(bound, max(-(-total // amount), total * loads[0] // sum(loads)))
    least = 1 if total - largest >= amount - 1 else 0
    counts, spare = [largest] + [least] * (amount - 1), total - largest - least * (amount - 1)
    while spare > 0:
        candidates = [i for i in range(1, amount) if counts[i] < largest] or [i for i in range(1, amount) if counts[i] < bound]
        whole, left = sum([loads[i] for i in candidates]), spare
        for i in candidates:
            extra = min(bound - counts[i], max(1, left * loads[i] // whole), spare)
            counts[i] = counts[i] + extra
            spare = spare - extra
    return np.array(counts)


def bell_draw(key, extent, scale, reach, split=(), held_as=jnp.bfloat16):
    loudness = block_levels(key, extent, split, -0.22, 0.18) if split else 1.0
    values = jax.random.normal(key, extent, jnp.float32) * scale * loudness
    return jnp.minimum(jnp.maximum(values, -reach), reach).astype(held_as)


def bell_draw_with(stream_key, extent, spread, bound, shards, heavy, kind=jnp.bfloat16):
    array = spread * jax.random.normal(stream_key, extent, jnp.float32)
    if shards:
        array = array * block_levels(stream_key, extent, shards, -0.22, 0.18)
    return jnp.clip(with_spikes(array, jax.random.fold_in(stream_key, 3), *heavy), -bound, bound).astype(kind)


def setup_inputs(seed: int = 0) -> dict:
    arg_keys = jax.random.split(jax.random.key(seed), 11)
    tokens = bell_draw(arg_keys[0], (TOKENS, D), 1.0, 6.0, ((0, 8), (1, 64)))
    cotangent = bell_draw(arg_keys[1], (TOKENS, D), 1.0, 6.0, ((0, 8), (1, 64)))
    expert_ids_keys = jax.random.split(jax.random.fold_in(arg_keys[2], 1), TOKENS // TOK_DEV)
    expert_ids_turns = jax.random.permutation(jax.random.fold_in(arg_keys[2], 3), TOKENS // TOK_DEV)
    expert_ids = jax.vmap(lambda own, number: assign_block(jax.random.fold_in(arg_keys[2], 2), own, number, TOK_DEV, EXPERTS, 2, CAP, 2))(expert_ids_keys, expert_ids_turns).reshape((TOKENS, TOP))
    route_weights = jnp.clip(0.2 + 0.8 * jax.random.uniform(arg_keys[3], (TOKENS, TOP), jnp.float32) ** block_levels(arg_keys[3], (TOKENS, TOP), ((0, 8),), -0.2, 0.2), 0.2, 1.0)
    dense_gate = bell_draw(arg_keys[4], (D, FF), D ** -0.5, 0.125, ((0, 8), (1, 64)))
    dense_up = bell_draw(arg_keys[5], (D, FF), D ** -0.5, 0.125, ((0, 8), (1, 64)))
    dense_down = bell_draw_with(arg_keys[6], (FF, D), FFW ** -0.5, 0.15625, ((0, 64), (1, 8)), (0, 1, 64, 4.0))
    noise_gate = bell_draw(arg_keys[7], (EXPERTS, D, FFW - FF), D ** -0.5, 0.125, ((0, 8), (2, 64)))
    noise_up = bell_draw(arg_keys[8], (EXPERTS, D, FFW - FF), D ** -0.5, 0.125, ((0, 8), (2, 64)))
    noise_down = bell_draw(arg_keys[9], (EXPERTS, FFW - FF, D), FFW ** -0.5, 0.0546875, ((0, 8), (1, 64)))
    return dict(tokens=tokens, cotangent=cotangent, expert_ids=expert_ids, route_weights=route_weights, dense_gate=dense_gate, dense_up=dense_up, dense_down=dense_down, noise_gate=noise_gate, noise_up=noise_up, noise_down=noise_down)


def reference(tokens, cotangent, expert_ids, route_weights, dense_gate, dense_up, dense_down, noise_gate, noise_up, noise_down):
    dense_block = FF // N_SHARD
    new_block = (FFW - FF) // N_SHARD
    rows_total = EXPERTS * CAP
    pair_ids = expert_ids.reshape(EXPERTS, 2 * TOK_DEV)
    onehot = (pair_ids[:, :, None] == jnp.arange(EXPERTS, dtype=jnp.int32)[None, None, :]).astype(jnp.int32)
    earlier = jnp.cumsum(onehot, axis=1) - onehot
    slot_index = jnp.sum(earlier * onehot, axis=2).astype(jnp.int32)
    block_index = jnp.arange(EXPERTS, dtype=jnp.int32)[:, None]
    row_index = (block_index * CAP + slot_index).reshape(-1).astype(jnp.int32)
    pair_expert = pair_ids.reshape(-1).astype(jnp.int32)
    flat_weights = route_weights.reshape(-1)
    tok_pairs = jnp.repeat(tokens, 2, axis=0)
    cot_pairs = (flat_weights[:, None] * jnp.repeat(cotangent, 2, axis=0).astype(jnp.float32)).astype(jnp.bfloat16)
    dispatched = jnp.zeros((EXPERTS, rows_total, D), jnp.bfloat16).at[pair_expert, row_index].set(tok_pairs)
    slot_grads = jnp.zeros((EXPERTS, rows_total, D), jnp.bfloat16).at[pair_expert, row_index].set(cot_pairs)
    outputs = []
    gate_list = []
    up_list = []
    down_list = []
    for expert in range(EXPERTS):
        wide_gate = jnp.concatenate([dense_gate.reshape(D, N_SHARD, dense_block), noise_gate[expert].reshape(D, N_SHARD, new_block)], axis=2).reshape(D, FFW)
        wide_up = jnp.concatenate([dense_up.reshape(D, N_SHARD, dense_block), noise_up[expert].reshape(D, N_SHARD, new_block)], axis=2).reshape(D, FFW)
        wide_down = jnp.concatenate([dense_down.reshape(N_SHARD, dense_block, D), noise_down[expert].reshape(N_SHARD, new_block, D)], axis=1).reshape(FFW, D)
        inputs = dispatched[expert]
        grads_in = slot_grads[expert]
        gate_pre = jnp.dot(inputs, wide_gate, preferred_element_type=jnp.float32)
        up_pre = jnp.dot(inputs, wide_up, preferred_element_type=jnp.float32)
        sigmoid_gate = jax.nn.sigmoid(gate_pre)
        silu_gate = gate_pre * sigmoid_gate
        hidden = (silu_gate * up_pre).astype(jnp.bfloat16)
        outputs.append(jnp.dot(hidden, wide_down, preferred_element_type=jnp.float32).astype(jnp.bfloat16))
        grad_hidden = jnp.dot(grads_in, wide_down.T, preferred_element_type=jnp.float32)
        grad_gate_pre = (grad_hidden * up_pre * sigmoid_gate * (1.0 + gate_pre * (1.0 - sigmoid_gate))).astype(jnp.bfloat16)
        grad_up_pre = (grad_hidden * silu_gate).astype(jnp.bfloat16)
        gate_list.append(jnp.dot(grad_gate_pre.T, inputs, preferred_element_type=jnp.float32).astype(jnp.bfloat16))
        up_list.append(jnp.dot(grad_up_pre.T, inputs, preferred_element_type=jnp.float32).astype(jnp.bfloat16))
        down_list.append(jnp.dot(hidden.T, grads_in, preferred_element_type=jnp.float32).astype(jnp.bfloat16))
    expert_out = jnp.stack(outputs)
    picked = expert_out[pair_expert, row_index].astype(jnp.float32)
    mixed = jnp.sum((picked * flat_weights[:, None]).reshape(TOKENS, 2, D), axis=1).astype(jnp.bfloat16)
    return mixed, jnp.stack(gate_list), jnp.stack(up_list), jnp.stack(down_list)
```

```python
import jax
import jax.numpy as jnp
from jax import lax
from jax.experimental import pallas as pl
from jax.experimental.pallas import tpu as pltpu
from jax.sharding import Mesh, PartitionSpec as P

BF = jnp.bfloat16
F32 = jnp.float32
ZH, NX, NY, ZL, NC = 2, 4, 4, 8, 2
CAP = 48
SLOT = 128
NT = (((1,), (1,)), ((), ()))
VM = pl.BlockSpec(memory_space=pltpu.VMEM)
SM = pl.BlockSpec(memory_space=pltpu.SMEM)


def call(kernel, out_shape, in_specs, scratch=()):
    return pl.pallas_call(
        kernel,
        out_shape=out_shape,
        in_specs=in_specs,
        out_specs=jax.tree.map(lambda _: VM, out_shape),
        scratch_shapes=scratch,
        compiler_params=pltpu.CompilerParams(vmem_limit_bytes=60000 * 1024),
    )


def sds(shape, dtype):
    return jax.ShapeDtypeStruct(shape, dtype)


def select_kernel(zh_ref, r_ref, send_ref, pick_ref, wt_ref):
    zh = zh_ref[0]
    row8 = lax.broadcasted_iota(jnp.int32, (8, 128), 0)
    expert = jnp.where(row8 < NX, zh * NX + row8, -1).astype(F32)
    before = (
        lax.broadcasted_iota(jnp.int32, (128, 128), 0)
        < lax.broadcasted_iota(jnp.int32, (128, 128), 1)
    ).astype(F32).astype(BF)
    slot = lax.broadcasted_iota(jnp.int32, (CAP, 128), 0).astype(F32)
    pick_ref[...] = jnp.zeros_like(pick_ref)
    wt_ref[...] = jnp.zeros_like(wt_ref)
    for b in range(ZH):
        meta = r_ref[b * ZL, 64:72, :].astype(F32)
        id0, id1 = meta[0:1], meta[1:2]
        w0 = meta[2:3] + meta[3:4] + meta[4:5]
        w1 = meta[5:6] + meta[6:7] + meta[7:8]
        is0 = expert == id0
        is1 = expert == id1
        member = jnp.where(is0 | is1, 1.0, 0.0)
        weight = jnp.where(is0, w0, jnp.where(is1, w1, 0.0))
        earlier = jnp.dot(member.astype(BF), before, preferred_element_type=F32)
        wt_ref[b] = weight
        tok = r_ref[b * ZL : (b + 1) * ZL, 0:32, :].reshape(ZL * 32, 128)
        cot = r_ref[b * ZL : (b + 1) * ZL, 32:64, :].reshape(ZL * 32, 128)
        for x in range(NX):
            hit = jnp.where(
                (member[x : x + 1] > 0.5) & (earlier[x : x + 1] == slot), 1.0, 0.0
            )
            wslot = jnp.sum(hit * weight[x : x + 1], axis=1, keepdims=True)
            one = hit.astype(BF)
            pick_ref[b, x, b * CAP : (b + 1) * CAP, :] = one
            st = lax.dot_general(one, tok, NT, preferred_element_type=F32).astype(BF)
            sc = lax.dot_general(one, cot, NT, preferred_element_type=F32)
            sc = (sc * wslot).astype(BF)
            for y in range(NY):
                send_ref[x * NY + y, b * CAP : (b + 1) * CAP, 0:256] = st
                send_ref[x * NY + y, b * CAP : (b + 1) * CAP, 256:512] = sc


def main_kernel(
    c_ref, own_ref, oth_ref, w_ref, part_ref, away_ref, gg_ref, gu_ref, gd_ref, in_s, sg_s, o_s
):
    c = c_ref[0]
    j = lax.broadcasted_iota(jnp.int32, (512, 512), 0)
    f = lax.broadcasted_iota(jnp.int32, (512, 512), 1)
    core = (f >> 5) & 1
    src = jnp.where(core == c, 0, 256) + ((f >> 6) << 5) + (f & 31)
    perm = jnp.where(j == src, 1.0, 0.0).astype(BF)
    for x in range(NX):
        in_s[x * SLOT + 96 : (x + 1) * SLOT, :] = jnp.zeros((32, 2048), BF)
        sg_s[x * SLOT + 96 : (x + 1) * SLOT, :] = jnp.zeros((32, 2048), BF)
        for y in range(NY):
            k = x * NY + y
            for at, dst in ((0, in_s), (256, sg_s)):
                both = jnp.concatenate(
                    [own_ref[k, :, at : at + 256], oth_ref[k, :, at : at + 256]], axis=1
                )
                dst[x * SLOT : x * SLOT + 96, y * 512 : (y + 1) * 512] = jnp.dot(
                    both, perm, preferred_element_type=F32
                ).astype(BF)
    inp = in_s[...]
    sg = sg_s[...]
    gate = lax.dot_general(w_ref[0], inp, NT, preferred_element_type=F32)
    up = lax.dot_general(w_ref[1], inp, NT, preferred_element_type=F32)
    sig = jax.nn.sigmoid(gate)
    silu = gate * sig
    hidden = (silu * up).astype(BF)
    o_s[...] = lax.dot_general(
        w_ref[2], hidden, (((0,), (0,)), ((), ())), preferred_element_type=F32
    ).reshape(32, 2, 32, NX * SLOT)
    part_ref[...] = o_s[:, pl.ds(c, 1)].reshape(32, 32, NX * SLOT)
    away_ref[...] = o_s[:, pl.ds(1 - c, 1)].reshape(32, 32, NX * SLOT).astype(BF)
    gh = lax.dot_general(w_ref[2], sg, NT, preferred_element_type=F32)
    ggp = (gh * up * sig * (1.0 + gate * (1.0 - sig))).astype(BF)
    gup = (gh * silu).astype(BF)
    gg_ref[...] = jnp.dot(ggp, inp, preferred_element_type=F32).astype(BF)
    gu_ref[...] = jnp.dot(gup, inp, preferred_element_type=F32).astype(BF)
    gd_ref[...] = jnp.dot(hidden, sg, preferred_element_type=F32).astype(BF)


def add_kernel(part_ref, got_ref, send_ref):
    for x in range(NX):
        for y in range(NY):
            a = part_ref[y * ZL : (y + 1) * ZL, :, x * SLOT : (x + 1) * SLOT]
            b = got_ref[y * ZL : (y + 1) * ZL, :, x * SLOT : (x + 1) * SLOT]
            send_ref[x * NY + y] = (a + b.astype(F32)).astype(BF).reshape(256, SLOT)


def combine_kernel(r_ref, pick_ref, wt_ref, send_ref):
    acc = [jnp.zeros((256, 128), F32) for _ in range(ZH)]
    for x in range(NX):
        s = r_ref[x * NY].astype(F32)
        for y in range(1, NY):
            s = s + r_ref[x * NY + y].astype(F32)
        hi = s.astype(BF)
        lo = (s - hi.astype(F32)).astype(BF)
        for b in range(ZH):
            one = pick_ref[b, x]
            g = jnp.dot(hi, one, preferred_element_type=F32) + jnp.dot(
                lo, one, preferred_element_type=F32
            )
            acc[b] = acc[b] + g * wt_ref[b, x : x + 1, :]
    for b in range(ZH):
        send_ref[b * ZL : (b + 1) * ZL] = acc[b].astype(BF).reshape(ZL, 32, 128)


def last_kernel(r_ref, o_ref):
    s = r_ref[0].astype(F32)
    for k in range(1, ZH * ZL):
        s = s + r_ref[k].astype(F32)
    o_ref[...] = s.T.astype(BF)


def swap(v, axis):
    return lax.ppermute(v, axis, [(0, 1), (1, 0)])


def exchange(v, axes):
    return lax.all_to_all(v, axes, 0, 0, tiled=True)


def local(
    tokens,
    cotangent,
    expert_ids,
    route_weights,
    dense_gate,
    dense_up,
    dense_down,
    noise_gate,
    noise_up,
    noise_down,
):
    zh = lax.axis_index("zh")
    zh_arr = zh.reshape(1).astype(jnp.int32)
    c_arr = lax.axis_index("c").reshape(1).astype(jnp.int32)

    mine = jnp.stack([dense_gate.T, dense_up.T, dense_down])
    theirs = swap(mine, "zh")

    w_t = route_weights.T
    hi = lax.reduce_precision(w_t, 8, 7)
    mid = lax.reduce_precision(w_t - hi, 8, 7)
    low = w_t - hi - mid
    meta = jnp.concatenate(
        [
            expert_ids.T.astype(BF),
            jnp.stack([hi, mid, low], axis=1).reshape(6, 128).astype(BF),
        ],
        axis=0,
    )
    payload = jnp.concatenate([tokens.T, cotangent.T, meta], axis=0)
    got = exchange(jnp.broadcast_to(payload[None], (ZH * ZL, 72, 128)), ("zh", "zl"))

    send, pick, wt = call(
        select_kernel,
        (
            sds((NX * NY, 96, 512), BF),
            sds((ZH, NX, SLOT, 128), BF),
            sds((ZH, 8, 128), F32),
        ),
        [SM, VM],
    )(zh_arr, got)
    w_near = exchange(jnp.broadcast_to(mine[None], (NX, *mine.shape)), "x")
    own = exchange(send, ("x", "y"))
    w_far = exchange(jnp.broadcast_to(theirs[None], (NX, *mine.shape)), "x")
    oth = swap(own, "c")

    first = jnp.where(zh == 0, w_near, w_far)
    second = jnp.where(zh == 0, w_far, w_near)
    dense = jnp.concatenate([first, second], axis=0)
    dense = dense.transpose(1, 2, 0, 3).reshape(3, mine.shape[1], 2048)
    noise = jnp.stack([noise_gate[0].T, noise_up[0].T, noise_down[0]])
    wide = jnp.concatenate([dense, noise], axis=1)
    hid = wide.shape[1]

    part, away, gg, gu, gd = call(
        main_kernel,
        (
            sds((32, 32, NX * SLOT), F32),
            sds((32, 32, NX * SLOT), BF),
            sds((hid, 2048), BF),
            sds((hid, 2048), BF),
            sds((hid, 2048), BF),
        ),
        [SM, VM, VM, VM],
        [
            pltpu.VMEM((NX * SLOT, 2048), BF),
            pltpu.VMEM((NX * SLOT, 2048), BF),
            pltpu.VMEM((32, 2, 32, NX * SLOT), F32),
        ],
    )(c_arr, own, oth, wide)
    back = swap(away, "c")
    send = call(add_kernel, sds((NX * NY, 256, SLOT), BF), [VM, VM])(part, back)
    got = exchange(send, ("x", "y"))
    send = call(combine_kernel, sds((ZH * ZL, 32, 128), BF), [VM, VM, VM])(got, pick, wt)
    got = exchange(send, ("zh", "zl"))
    mixed = call(last_kernel, sds((128, 32), BF), [VM])(got)
    return mixed, gg[None], gu[None], gd[None]


def solution(mesh):
    e, s = ("zh", "x"), ("y", "zl", "c")
    fine = Mesh(mesh.devices.reshape(ZH, NX, NY, ZL, NC), e + s)
    in_specs = (
        P(e, s),
        P(e, s),
        P(e, None),
        P(e, None),
        P(e, s),
        P(e, s),
        P(s, e),
        P(e, None, s),
        P(e, None, s),
        P(e, s, None),
    )
    out_specs = (P(e, s), P(e, s, None), P(e, s, None), P(e, s, None))
    return jax.shard_map(local, mesh=fine, in_specs=in_specs, out_specs=out_specs, check_vma=False)
```

```python
import jax
import jax.numpy as jnp
from jax import lax
from jax.experimental import pallas as pl
from jax.experimental.pallas import tpu as pltpu
from jax.sharding import Mesh, PartitionSpec as P

BF = jnp.bfloat16
F32 = jnp.float32
ZH, NX, NY, ZL, NC = 2, 4, 4, 8, 2
CAP = 48
ROWS = 2 * CAP
NT = (((1,), (1,)), ((), ()))
VM = pl.BlockSpec(memory_space=pltpu.VMEM)
SM = pl.BlockSpec(memory_space=pltpu.SMEM)


def call(kernel, out_shape, in_specs, scratch=(), mib=8, flops=0):
    return pl.pallas_call(
        kernel,
        out_shape=out_shape,
        in_specs=in_specs,
        out_specs=jax.tree.map(lambda _: VM, out_shape),
        scratch_shapes=scratch,
        compiler_params=pltpu.CompilerParams(vmem_limit_bytes=mib * 1024 * 1024),
    )


def sds(shape, dtype):
    return jax.ShapeDtypeStruct(shape, dtype)


def pack_kernel(tok_ref, cot_ref, id_ref, w_ref, a_ref):
    w = w_ref[...]
    high = w.astype(BF).astype(F32)
    mid = (w - high).astype(BF).astype(F32)
    low = w - high - mid
    meta = jnp.concatenate([id_ref[...].astype(F32), high, mid, low], axis=0).astype(BF)
    for k in range(ZH * ZL):
        a_ref[k, 0:32, :] = tok_ref[...]
        a_ref[k, 32:64, :] = cot_ref[...]
        a_ref[k, 64:72, :] = meta


def select_kernel(at_ref, r_ref, tok_ref, cot_ref, back_ref, ws_ref):
    zh = at_ref[0]
    row8 = lax.broadcasted_iota(jnp.int32, (8, 128), 0)
    expert = jnp.where(row8 < NX, zh * NX + row8, -1).astype(F32)
    before = (
        lax.broadcasted_iota(jnp.int32, (128, 128), 0)
        < lax.broadcasted_iota(jnp.int32, (128, 128), 1)
    ).astype(F32).astype(BF)
    slot = lax.broadcasted_iota(jnp.int32, (CAP, 128), 0).astype(F32)
    for b in range(ZH):
        meta = r_ref[b * ZL, 64:72, :].astype(F32)
        id0, id1 = meta[0:1], meta[1:2]
        w0 = meta[2:3] + meta[4:5] + meta[6:7]
        w1 = meta[3:4] + meta[5:6] + meta[7:8]
        is0 = expert == id0
        is1 = expert == id1
        member = jnp.where(is0 | is1, 1.0, 0.0)
        weight = jnp.where(is0, w0, jnp.where(is1, w1, 0.0))
        earlier = jnp.dot(member.astype(BF), before, preferred_element_type=F32)
        hits, ws = [], []
        for x in range(NX):
            hit = jnp.where(
                (member[x : x + 1] > 0.5) & (earlier[x : x + 1] == slot), 1.0, 0.0
            )
            hits.append(hit)
            ws.append(jnp.sum(hit * weight[x : x + 1], axis=1, keepdims=True))
        hit = jnp.concatenate(hits, axis=0)
        wslot = jnp.concatenate(ws, axis=0)
        one = hit.astype(BF)
        back_ref[b] = hit.T.astype(BF)
        ws_ref[b] = jnp.broadcast_to(wslot, (NX * CAP, 128))
        for at, scale, dst in ((0, None, tok_ref), (32, wslot, cot_ref)):
            v = r_ref[b * ZL : (b + 1) * ZL, at : at + 32, :].reshape(ZL * 32, 128)
            v = lax.dot_general(one, v, NT, preferred_element_type=F32)
            v = (v if scale is None else v * scale).astype(BF)
            for x in range(NX):
                for y in range(NY):
                    dst[x * NY + y, b * CAP : (b + 1) * CAP, :] = v[x * CAP : (x + 1) * CAP]


def spread(c):
    j = lax.broadcasted_iota(jnp.int32, (512, 512), 0)
    f = lax.broadcasted_iota(jnp.int32, (512, 512), 1)
    src = jnp.where(((f >> 5) & 1) == c, 0, 256) + ((f >> 6) << 5) + (f & 31)
    return jnp.where(j == src, 1.0, 0.0).astype(BF)


def join(own_ref, oth_ref, perm, dst):
    for y in range(NY):
        rows = jnp.concatenate(
            [
                jnp.concatenate([own_ref[x * NY + y], oth_ref[x * NY + y]], axis=1)
                for x in range(NX)
            ],
            axis=0,
        )
        dst[:, y * 512 : (y + 1) * 512] = jnp.dot(
            rows, perm, preferred_element_type=F32
        ).astype(BF)


HID = 208
DENSE, NEW_AT, NEW = 172, 176, 20


def forward_kernel(
    at_ref, own_ref, oth_ref, n0, n1, n2, n3, f0, f1, f2, f3, ng_ref, nu_ref, nd_ref,
    part_ref, away_ref, in_ref, gu_ref, hid_ref, down_ref, w_s,
):
    zh, c, at_x = at_ref[0], at_ref[1], at_ref[2]
    perm = spread(c)
    join(own_ref, oth_ref, perm, in_ref)
    for m, new in ((0, ng_ref), (1, nu_ref)):
        w_s[m, 160:HID, :] = jnp.zeros((HID - 160, 2048), BF)
        w_s[m, NEW_AT : NEW_AT + NEW, :] = new[...]
    down_ref[160:HID, :] = jnp.zeros((HID - 160, 2048), BF)
    down_ref[NEW_AT : NEW_AT + NEW, :] = nd_ref[...]
    for half, refs in ((zh, (n0, n1, n2, n3)), (1 - zh, (f0, f1, f2, f3))):
        for k, ref in enumerate(refs):
            source = half * NX + ((at_x + NX - k) & (NX - 1))
            lanes = pl.ds(pl.multiple_of(source * 256, 256), 256)
            w_s[0, 0:DENSE, lanes] = ref[0]
            w_s[1, 0:DENSE, lanes] = ref[1]
            down_ref[0:DENSE, lanes] = ref[2]
    gu = lax.dot_general(
        w_s[...].reshape(2 * HID, 2048), in_ref[...], NT, preferred_element_type=F32
    )
    gu_ref[...] = gu
    gate, up = gu[0:HID], gu[HID : 2 * HID]
    hidden = gate * jax.nn.sigmoid(gate) * up
    hid_ref[...] = hidden.astype(BF)
    rows = hidden.T.astype(BF)
    for y in range(NY):
        d = lax.dot_general(
            down_ref[:, y * 512 : (y + 1) * 512], perm, NT, preferred_element_type=F32
        ).astype(BF)
        o = jnp.dot(rows, d, preferred_element_type=F32)
        for x in range(NX):
            part_ref[x * NY + y] = o[x * ROWS : (x + 1) * ROWS, 0:256]
            away_ref[x * NY + y] = o[x * ROWS : (x + 1) * ROWS, 256:512].astype(BF)


def grad_kernel(
    at_ref, own_ref, oth_ref, in_ref, gu_ref, hid_ref, down_ref, gg_ref, gup_ref, gd_ref, sg_s
):
    join(own_ref, oth_ref, spread(at_ref[1]), sg_s)
    sg = sg_s[...]
    inp = in_ref[...]
    gate, up = gu_ref[0:HID], gu_ref[HID : 2 * HID]
    sig = jax.nn.sigmoid(gate)
    gh = lax.dot_general(down_ref[...], sg, NT, preferred_element_type=F32)
    ggp = (gh * up * sig * (1.0 + gate * (1.0 - sig))).astype(BF)
    gup = (gh * (gate * sig)).astype(BF)
    for lhs, rhs, out in ((ggp, inp, gg_ref), (gup, inp, gup_ref), (hid_ref[...], sg, gd_ref)):
        g = jnp.dot(lhs, rhs, preferred_element_type=F32).astype(BF)
        out[0:DENSE, :] = g[0:DENSE]
        out[DENSE : DENSE + NEW, :] = g[NEW_AT : NEW_AT + NEW]


def combine_kernel(r_ref, back_ref, ws_ref, send_ref):
    sums = []
    for x in range(NX):
        s = r_ref[x * NY].astype(F32)
        for y in range(1, NY):
            s = s + r_ref[x * NY + y].astype(F32)
        sums.append(s)
    for b in range(ZH):
        s = jnp.concatenate([v[b * CAP : (b + 1) * CAP] for v in sums], axis=0)
        s = s * ws_ref[b, :, 0:1]
        hi = s.astype(BF)
        lo = (s - hi.astype(F32)).astype(BF)
        m = jnp.dot(back_ref[b], hi, preferred_element_type=F32) + jnp.dot(
            back_ref[b], lo, preferred_element_type=F32
        )
        send_ref[b * ZL : (b + 1) * ZL] = m.T.astype(BF).reshape(ZL, 32, 128)


def swap(v, axis):
    return lax.ppermute(v, axis, [(0, 1), (1, 0)])


def turn(v, k):
    return lax.ppermute(v, "x", [(i, (i + k) % NX) for i in range(NX)])


def exchange(v, axes):
    return lax.all_to_all(v, axes, 0, 0, tiled=True)


def local(
    tokens,
    cotangent,
    expert_ids,
    route_weights,
    dense_gate,
    dense_up,
    dense_down,
    noise_gate,
    noise_up,
    noise_down,
):
    Z, XY = ("zh", "zl"), ("x", "y")
    at = jnp.stack([lax.axis_index(n) for n in ("zh", "c", "x")]).astype(jnp.int32)
    hid = dense_down.shape[0] + noise_down.shape[1]

    mine = jnp.stack([dense_gate.T, dense_up.T, dense_down])
    theirs = swap(mine, "zh")
    payload = call(pack_kernel, sds((16, 72, 128), BF), [VM] * 4)(
        tokens.T, cotangent.T, expert_ids.T, route_weights.T
    )
    near = [mine] + [turn(mine, k) for k in range(1, NX)]
    got = exchange(payload, Z)
    got, theirs, near = lax.optimization_barrier((got, theirs, near))
    tok_send, cot_send, back, ws = call(
        select_kernel,
        (
            sds((16, ROWS, 256), BF),
            sds((16, ROWS, 256), BF),
            sds((ZH, 128, NX * CAP), BF),
            sds((ZH, NX * CAP, 128), F32),
        ),
        [SM, VM],
    )(at, got)
    own = exchange(tok_send, XY)
    far = [theirs] + [turn(theirs, k) for k in range(1, NX)]
    oth = swap(own, "c")
    cot_send, _ = lax.optimization_barrier((cot_send, own))
    own_cot = exchange(cot_send, XY)
    oth_cot = swap(own_cot, "c")

    part, away, inp, gu, hidden, down = call(
        forward_kernel,
        (
            sds((16, ROWS, 256), F32),
            sds((16, ROWS, 256), BF),
            sds((NX * ROWS, 2048), BF),
            sds((2 * HID, NX * ROWS), F32),
            sds((HID, NX * ROWS), BF),
            sds((HID, 2048), BF),
        ),
        [SM] + [VM] * 13,
        [pltpu.VMEM((2, HID, 2048), BF)],
        mib=28,
    )(at, own, oth, *near, *far, noise_gate[0].T, noise_up[0].T, noise_down[0])
    send = (part + swap(away, "c").astype(F32)).astype(BF)
    own_cot, oth_cot, send = lax.optimization_barrier((own_cot, oth_cot, send))
    gg, gup, gd = call(
        grad_kernel,
        (sds((hid, 2048), BF),) * 3,
        [SM] + [VM] * 6,
        [pltpu.VMEM((NX * ROWS, 2048), BF)],
        mib=28,
    )(at, own_cot, oth_cot, inp, gu, hidden, down)
    got = exchange(send, XY)
    send = call(combine_kernel, sds((16, 32, 128), BF), [VM] * 3)(got, back, ws)
    got = exchange(send, Z)
    mixed = jnp.sum(got.astype(F32), axis=0).astype(BF).T
    return mixed, gg[None], gup[None], gd[None]


def solution(mesh):
    e, s = ("zh", "x"), ("y", "zl", "c")
    fine = Mesh(mesh.devices.reshape(ZH, NX, NY, ZL, NC), e + s)
    in_specs = (
        P(e, s),
        P(e, s),
        P(e, None),
        P(e, None),
        P(e, s),
        P(e, s),
        P(s, e),
        P(e, None, s),
        P(e, None, s),
        P(e, s, None),
    )
    out_specs = (P(e, s), P(e, s, None), P(e, s, None), P(e, s, None))
    return jax.shard_map(local, mesh=fine, in_specs=in_specs, out_specs=out_specs, check_vma=False)
```

```python
import jax
import jax.numpy as jnp
from jax import lax
from jax.experimental import pallas as pl
from jax.experimental.pallas import tpu as pltpu
from jax.sharding import Mesh, PartitionSpec as P

BF = jnp.bfloat16
F32 = jnp.float32
ZH, NX, NY, ZL, NC = 2, 4, 4, 8, 2
CAP = 48
ROWS = 2 * CAP
NT = (((1,), (1,)), ((), ()))
VM = pl.BlockSpec(memory_space=pltpu.VMEM)
HB = pl.BlockSpec(memory_space=pltpu.HBM)
SM = pl.BlockSpec(memory_space=pltpu.SMEM)


def call(body, out_shape, operands, scratch=(), mib=8, scalars=None, direct=None):
    n, m = len(operands), len(out_shape)

    def kernel(*refs):
        refs = list(refs)
        at = refs.pop(0) if scalars is not None else None
        ins, outs, rest = refs[:n], refs[n : n + m], refs[n + m :]
        in_bufs, out_bufs, rest = rest[:n], rest[n : n + m], rest[n + m :]
        in_sem, out_sem, rest = rest[0], rest[1], rest[2:]
        copies = {
            i: pltpu.make_async_copy(ins[i], in_bufs[i], in_sem.at[i])
            for i in range(n)
            if i != direct
        }
        for copy in copies.values():
            copy.start()

        def get(i):
            if i == direct:
                return ins[i]
            copies[i].wait()
            return in_bufs[i]

        written = []

        def put(i):
            copy = pltpu.make_async_copy(out_bufs[i], outs[i], out_sem.at[i])
            copy.start()
            written.append(copy)

        body(at, get, out_bufs, put, *rest)
        for copy in written:
            copy.wait()

    return pl.pallas_call(
        kernel,
        out_shape=tuple(pltpu.HBM(o.shape, o.dtype) for o in out_shape),
        in_specs=([SM] if scalars is not None else [])
        + [VM if i == direct else HB for i in range(n)],
        out_specs=(HB,) * m,
        scratch_shapes=[
            pltpu.VMEM((8, 128) if i == direct else o.shape, o.dtype)
            for i, o in enumerate(operands)
        ]
        + [pltpu.VMEM(o.shape, o.dtype) for o in out_shape]
        + [pltpu.SemaphoreType.DMA((n,)), pltpu.SemaphoreType.DMA((m,))]
        + list(scratch),
        compiler_params=pltpu.CompilerParams(vmem_limit_bytes=mib * 1024 * 1024),
    )(
        *(() if scalars is None else (scalars,)),
        *[
            o if i == direct else pltpu.with_memory_space_constraint(o, pltpu.HBM)
            for i, o in enumerate(operands)
        ],
    )


def sds(shape, dtype):
    return jax.ShapeDtypeStruct(shape, dtype)


def pack_kernel(at, get, outs, put):
    (a_ref,) = outs
    id_ref, w_ref, tok_ref, cot_ref = get(0), get(1), get(2), get(3)
    w = w_ref[...]
    high = w.astype(BF).astype(F32)
    mid = (w - high).astype(BF).astype(F32)
    low = w - high - mid
    meta = jnp.concatenate([id_ref[...].astype(F32), high, mid, low], axis=0).astype(BF)
    for k in range(ZH * ZL):
        a_ref[k, 0:32, :] = tok_ref[...]
        a_ref[k, 32:64, :] = cot_ref[...]
        a_ref[k, 64:72, :] = meta
    put(0)


def select_kernel(at_ref, get, outs, put):
    tok_ref, cot_ref, back_ref, ws_ref = outs
    r_ref = get(0)
    zh = at_ref[0]
    row8 = lax.broadcasted_iota(jnp.int32, (8, 128), 0)
    expert = jnp.where(row8 < NX, zh * NX + row8, -1).astype(F32)
    before = (
        lax.broadcasted_iota(jnp.int32, (128, 128), 0)
        < lax.broadcasted_iota(jnp.int32, (128, 128), 1)
    ).astype(F32).astype(BF)
    slot = lax.broadcasted_iota(jnp.int32, (CAP, 128), 0).astype(F32)
    for b in range(ZH):
        meta = r_ref[b * ZL, 64:72, :].astype(F32)
        id0, id1 = meta[0:1], meta[1:2]
        w0 = meta[2:3] + meta[4:5] + meta[6:7]
        w1 = meta[3:4] + meta[5:6] + meta[7:8]
        is0 = expert == id0
        is1 = expert == id1
        member = jnp.where(is0 | is1, 1.0, 0.0)
        weight = jnp.where(is0, w0, jnp.where(is1, w1, 0.0))
        earlier = jnp.dot(member.astype(BF), before, preferred_element_type=F32)
        hits, ws = [], []
        for x in range(NX):
            hit = jnp.where(
                (member[x : x + 1] > 0.5) & (earlier[x : x + 1] == slot), 1.0, 0.0
            )
            hits.append(hit)
            ws.append(jnp.sum(hit * weight[x : x + 1], axis=1, keepdims=True))
        hit = jnp.concatenate(hits, axis=0)
        wslot = jnp.concatenate(ws, axis=0)
        one = hit.astype(BF)
        back_ref[b] = hit.T.astype(BF)
        ws_ref[b] = jnp.broadcast_to(wslot, (NX * CAP, 128))
        for at, scale, dst in ((0, None, tok_ref), (32, wslot, cot_ref)):
            v = r_ref[b * ZL : (b + 1) * ZL, at : at + 32, :].reshape(ZL * 32, 128)
            v = lax.dot_general(one, v, NT, preferred_element_type=F32)
            v = (v if scale is None else v * scale).astype(BF)
            for x in range(NX):
                for y in range(NY):
                    dst[x * NY + y, b * CAP : (b + 1) * CAP, :] = v[x * CAP : (x + 1) * CAP]
    for i in range(4):
        put(i)


def spread(c):
    j = lax.broadcasted_iota(jnp.int32, (512, 512), 0)
    f = lax.broadcasted_iota(jnp.int32, (512, 512), 1)
    src = jnp.where(((f >> 5) & 1) == c, 0, 256) + ((f >> 6) << 5) + (f & 31)
    return jnp.where(j == src, 1.0, 0.0).astype(BF)


def join(own_ref, oth_ref, perm, dst):
    for y in range(NY):
        rows = jnp.concatenate(
            [
                jnp.concatenate([own_ref[x * NY + y], oth_ref[x * NY + y]], axis=1)
                for x in range(NX)
            ],
            axis=0,
        )
        dst[:, y * 512 : (y + 1) * 512] = jnp.dot(
            rows, perm, preferred_element_type=F32
        ).astype(BF)


HID = 208
DENSE, NEW_AT, NEW = 172, 176, 20


def forward_kernel(at_ref, get, outs, put, w_s):
    part_ref, away_ref, in_ref, gu_ref, hid_ref, down_ref = outs
    zh, c, at_x = at_ref[0], at_ref[1], at_ref[2]
    perm = spread(c)
    join(get(0), get(1), perm, in_ref)
    put(2)
    ng_ref, nu_ref, nd_ref = get(10), get(11), get(12)
    for m, new in ((0, ng_ref), (1, nu_ref)):
        w_s[m, 160:HID, :] = jnp.zeros((HID - 160, 2048), BF)
        w_s[m, NEW_AT : NEW_AT + NEW, :] = new[...]
    down_ref[160:HID, :] = jnp.zeros((HID - 160, 2048), BF)
    down_ref[NEW_AT : NEW_AT + NEW, :] = nd_ref[...]
    for first, half in ((2, zh), (6, 1 - zh)):
        for k in range(NX):
            ref = get(first + k)
            source = half * NX + ((at_x + NX - k) & (NX - 1))
            lanes = pl.ds(pl.multiple_of(source * 256, 256), 256)
            w_s[0, 0:DENSE, lanes] = ref[0]
            w_s[1, 0:DENSE, lanes] = ref[1]
            down_ref[0:DENSE, lanes] = ref[2]
    put(5)
    gu = lax.dot_general(
        w_s[...].reshape(2 * HID, 2048), in_ref[...], NT, preferred_element_type=F32
    )
    gu_ref[...] = gu
    put(3)
    gate, up = gu[0:HID], gu[HID : 2 * HID]
    hidden = gate * jax.nn.sigmoid(gate) * up
    hid_ref[...] = hidden.astype(BF)
    put(4)
    rows = hidden.T.astype(BF)
    for y in range(NY):
        d = lax.dot_general(
            down_ref[:, y * 512 : (y + 1) * 512], perm, NT, preferred_element_type=F32
        ).astype(BF)
        o = jnp.dot(rows, d, preferred_element_type=F32)
        for x in range(NX):
            part_ref[x * NY + y] = o[x * ROWS : (x + 1) * ROWS, 0:256]
            away_ref[x * NY + y] = o[x * ROWS : (x + 1) * ROWS, 256:512].astype(BF)
    put(1)
    put(0)


def grad_kernel(at_ref, get, outs, put, sg_s):
    join(get(0), get(1), spread(at_ref[1]), sg_s)
    in_ref, gu_ref, hid_ref, down_ref = get(2), get(3), get(4), get(5)
    sg = sg_s[...]
    inp = in_ref[...]
    gate, up = gu_ref[0:HID], gu_ref[HID : 2 * HID]
    sig = jax.nn.sigmoid(gate)
    gh = lax.dot_general(down_ref[...], sg, NT, preferred_element_type=F32)
    ggp = (gh * up * sig * (1.0 + gate * (1.0 - sig))).astype(BF)
    gup = (gh * (gate * sig)).astype(BF)
    for i, (lhs, rhs) in enumerate(((hid_ref[...], sg), (ggp, inp), (gup, inp))):
        out = outs[i]
        g = jnp.dot(lhs, rhs, preferred_element_type=F32).astype(BF)
        out[0:DENSE, :] = g[0:DENSE]
        out[DENSE : DENSE + NEW, :] = g[NEW_AT : NEW_AT + NEW]
        put(i)


def combine_kernel(at, get, outs, put):
    (send_ref,) = outs
    r_ref, back_ref, ws_ref = get(0), get(1), get(2)
    sums = []
    for x in range(NX):
        s = r_ref[x * NY].astype(F32)
        for y in range(1, NY):
            s = s + r_ref[x * NY + y].astype(F32)
        sums.append(s)
    for b in range(ZH):
        s = jnp.concatenate([v[b * CAP : (b + 1) * CAP] for v in sums], axis=0)
        s = s * ws_ref[b, :, 0:1]
        hi = s.astype(BF)
        lo = (s - hi.astype(F32)).astype(BF)
        m = jnp.dot(back_ref[b], hi, preferred_element_type=F32) + jnp.dot(
            back_ref[b], lo, preferred_element_type=F32
        )
        send_ref[b * ZL : (b + 1) * ZL] = m.T.astype(BF).reshape(ZL, 32, 128)
    put(0)


def swap(v, axis):
    return lax.ppermute(v, axis, [(0, 1), (1, 0)])


def turn(v, k):
    return lax.ppermute(v, "x", [(i, (i + k) % NX) for i in range(NX)])


def exchange(v, axes):
    return lax.all_to_all(v, axes, 0, 0, tiled=True)


def local(
    tokens,
    cotangent,
    expert_ids,
    route_weights,
    dense_gate,
    dense_up,
    dense_down,
    noise_gate,
    noise_up,
    noise_down,
):
    Z, XY = ("zh", "zl"), ("x", "y")
    at = jnp.stack([lax.axis_index(n) for n in ("zh", "c", "x")]).astype(jnp.int32)
    hid = dense_down.shape[0] + noise_down.shape[1]

    mine = jnp.stack([dense_gate.T, dense_up.T, dense_down])
    theirs = swap(mine, "zh")
    mine, tokens = lax.optimization_barrier((mine, tokens))
    (payload,) = call(
        pack_kernel,
        [sds((16, 72, 128), BF)],
        [expert_ids.T, route_weights.T, tokens.T, cotangent.T],
    )
    near = [mine] + [turn(mine, k) for k in range(1, NX)]
    got = exchange(payload, Z)
    got, theirs = lax.optimization_barrier((got, theirs))
    tok_send, cot_send, back, ws = call(
        select_kernel,
        [
            sds((16, ROWS, 256), BF),
            sds((16, ROWS, 256), BF),
            sds((ZH, 128, NX * CAP), BF),
            sds((ZH, NX * CAP, 128), F32),
        ],
        [got],
        scalars=at,
        direct=0,
    )
    tok_send, near = lax.optimization_barrier((tok_send, near))
    own = exchange(tok_send, XY)
    far = [theirs] + [turn(theirs, k) for k in range(1, NX)]
    oth = swap(own, "c")
    own, far = lax.optimization_barrier((own, far))
    oth = swap(own, "c")
    cot_send, _ = lax.optimization_barrier((cot_send, own))
    own_cot = exchange(cot_send, XY)
    oth_cot = swap(own_cot, "c")

    part, away, inp, gu, hidden, down = call(
        forward_kernel,
        [
            sds((16, ROWS, 256), F32),
            sds((16, ROWS, 256), BF),
            sds((NX * ROWS, 2048), BF),
            sds((2 * HID, NX * ROWS), F32),
            sds((HID, NX * ROWS), BF),
            sds((HID, 2048), BF),
        ],
        [own, oth, *near, *far, noise_gate[0].T, noise_up[0].T, noise_down[0]],
        [pltpu.VMEM((2, HID, 2048), BF)],
        mib=32,
        scalars=at,
        direct=1,
    )
    send = (part + swap(away, "c").astype(F32)).astype(BF)
    own_cot, oth_cot, send = lax.optimization_barrier((own_cot, oth_cot, send))
    gd, gg, gup = call(
        grad_kernel,
        [sds((hid, 2048), BF)] * 3,
        [own_cot, oth_cot, inp, gu, hidden, down],
        [pltpu.VMEM((NX * ROWS, 2048), BF)],
        mib=32,
        scalars=at,
    )
    got = exchange(send, XY)
    (send,) = call(combine_kernel, [sds((16, 32, 128), BF)], [got, back, ws], direct=0)
    got = exchange(send, Z)
    mixed = jnp.sum(got.astype(F32), axis=0).astype(BF).T
    return mixed, gg[None], gup[None], gd[None]


def solution(mesh):
    e, s = ("zh", "x"), ("y", "zl", "c")
    fine = Mesh(mesh.devices.reshape(ZH, NX, NY, ZL, NC), e + s)
    in_specs = (
        P(e, s),
        P(e, s),
        P(e, None),
        P(e, None),
        P(e, s),
        P(e, s),
        P(s, e),
        P(e, None, s),
        P(e, None, s),
        P(e, s, None),
    )
    out_specs = (P(e, s), P(e, s, None), P(e, s, None), P(e, s, None))
    return jax.shard_map(local, mesh=fine, in_specs=in_specs, out_specs=out_specs, check_vma=False)
```

```python
import jax
import jax.numpy as jnp
from jax import lax
from jax.experimental import pallas as pl
from jax.experimental.pallas import tpu as pltpu
from jax.sharding import Mesh, PartitionSpec as P

BF = jnp.bfloat16
F32 = jnp.float32
ZH, NX, NY, ZL, NC = 2, 4, 4, 8, 2
CAP = 48
ROWS = 2 * CAP
NT = (((1,), (1,)), ((), ()))
VM = pl.BlockSpec(memory_space=pltpu.VMEM)
HB = pl.BlockSpec(memory_space=pltpu.HBM)
SM = pl.BlockSpec(memory_space=pltpu.SMEM)


def call(body, out_shape, operands, scratch=(), mib=8, scalars=None, direct=None):
    n, m = len(operands), len(out_shape)

    def kernel(*refs):
        refs = list(refs)
        at = refs.pop(0) if scalars is not None else None
        ins, outs, rest = refs[:n], refs[n : n + m], refs[n + m :]
        in_bufs, out_bufs, rest = rest[:n], rest[n : n + m], rest[n + m :]
        in_sem, out_sem, rest = rest[0], rest[1], rest[2:]
        copies = {
            i: pltpu.make_async_copy(ins[i], in_bufs[i], in_sem.at[i])
            for i in range(n)
            if i != direct
        }
        for copy in copies.values():
            copy.start()

        def get(i):
            if i == direct:
                return ins[i]
            copies[i].wait()
            return in_bufs[i]

        written = []

        def put(i):
            copy = pltpu.make_async_copy(out_bufs[i], outs[i], out_sem.at[i])
            copy.start()
            written.append(copy)

        body(at, get, out_bufs, put, *rest)
        for copy in written:
            copy.wait()

    return pl.pallas_call(
        kernel,
        out_shape=tuple(pltpu.HBM(o.shape, o.dtype) for o in out_shape),
        in_specs=([SM] if scalars is not None else [])
        + [VM if i == direct else HB for i in range(n)],
        out_specs=(HB,) * m,
        scratch_shapes=[
            pltpu.VMEM((8, 128) if i == direct else o.shape, o.dtype)
            for i, o in enumerate(operands)
        ]
        + [pltpu.VMEM(o.shape, o.dtype) for o in out_shape]
        + [pltpu.SemaphoreType.DMA((n,)), pltpu.SemaphoreType.DMA((m,))]
        + list(scratch),
        compiler_params=pltpu.CompilerParams(vmem_limit_bytes=mib * 1024 * 1024),
    )(
        *(() if scalars is None else (scalars,)),
        *[
            o if i == direct else pltpu.with_memory_space_constraint(o, pltpu.HBM)
            for i, o in enumerate(operands)
        ],
    )


def sds(shape, dtype):
    return jax.ShapeDtypeStruct(shape, dtype)


def pack_kernel(at, get, outs, put):
    (a_ref,) = outs
    id_ref, w_ref, tok_ref, cot_ref = get(0), get(1), get(2), get(3)
    w = w_ref[...]
    high = w.astype(BF).astype(F32)
    mid = (w - high).astype(BF).astype(F32)
    low = w - high - mid
    meta = jnp.concatenate([id_ref[...].astype(F32), high, mid, low], axis=0).astype(BF)
    for k in range(ZH * ZL):
        a_ref[k, 0:32, :] = tok_ref[...]
        a_ref[k, 32:64, :] = cot_ref[...]
        a_ref[k, 64:72, :] = meta
    put(0)


def select_kernel(at_ref, get, outs, put):
    tok_ref, cot_ref, back_ref, ws_ref = outs
    r_ref = get(0)
    zh = at_ref[0]
    row8 = lax.broadcasted_iota(jnp.int32, (8, 128), 0)
    expert = jnp.where(row8 < NX, zh * NX + row8, -1).astype(F32)
    before = (
        lax.broadcasted_iota(jnp.int32, (128, 128), 0)
        < lax.broadcasted_iota(jnp.int32, (128, 128), 1)
    ).astype(F32).astype(BF)
    slot = lax.broadcasted_iota(jnp.int32, (CAP, 128), 0).astype(F32)
    for b in range(ZH):
        meta = r_ref[b * ZL, 64:72, :].astype(F32)
        id0, id1 = meta[0:1], meta[1:2]
        w0 = meta[2:3] + meta[4:5] + meta[6:7]
        w1 = meta[3:4] + meta[5:6] + meta[7:8]
        is0 = expert == id0
        is1 = expert == id1
        member = jnp.where(is0 | is1, 1.0, 0.0)
        weight = jnp.where(is0, w0, jnp.where(is1, w1, 0.0))
        earlier = jnp.dot(member.astype(BF), before, preferred_element_type=F32)
        hits, ws = [], []
        for x in range(NX):
            hit = jnp.where(
                (member[x : x + 1] > 0.5) & (earlier[x : x + 1] == slot), 1.0, 0.0
            )
            hits.append(hit)
            ws.append(jnp.sum(hit * weight[x : x + 1], axis=1, keepdims=True))
        hit = jnp.concatenate(hits, axis=0)
        wslot = jnp.concatenate(ws, axis=0)
        one = hit.astype(BF)
        back_ref[b] = hit.T.astype(BF)
        ws_ref[b] = jnp.broadcast_to(wslot, (NX * CAP, 128))
        for at, scale, dst in ((0, None, tok_ref), (32, wslot, cot_ref)):
            v = r_ref[b * ZL : (b + 1) * ZL, at : at + 32, :].reshape(ZL * 32, 128)
            v = lax.dot_general(one, v, NT, preferred_element_type=F32)
            v = (v if scale is None else v * scale).astype(BF)
            for x in range(NX):
                for y in range(NY):
                    dst[x * NY + y, b * CAP : (b + 1) * CAP, :] = v[x * CAP : (x + 1) * CAP]
    for i in range(4):
        put(i)


def spread(c):
    j = lax.broadcasted_iota(jnp.int32, (512, 512), 0)
    f = lax.broadcasted_iota(jnp.int32, (512, 512), 1)
    src = jnp.where(((f >> 5) & 1) == c, 0, 256) + ((f >> 6) << 5) + (f & 31)
    return jnp.where(j == src, 1.0, 0.0).astype(BF)


def join(own_ref, oth_ref, perm, dst):
    for y in range(NY):
        rows = jnp.concatenate(
            [
                jnp.concatenate([own_ref[x * NY + y], oth_ref[x * NY + y]], axis=1)
                for x in range(NX)
            ],
            axis=0,
        )
        dst[:, y * 512 : (y + 1) * 512] = jnp.dot(
            rows, perm, preferred_element_type=F32
        ).astype(BF)


HID = 208
DENSE, NEW_AT, NEW = 172, 176, 20


def forward_kernel(at_ref, get, outs, put, w_s):
    part_ref, away_ref, in_ref, gu_ref, hid_ref, down_ref = outs
    zh, c, at_x = at_ref[0], at_ref[1], at_ref[2]
    perm = spread(c)
    join(get(0), get(1), perm, in_ref)
    put(2)
    ng_ref, nu_ref, nd_ref = get(10), get(11), get(12)
    for m, new in ((0, ng_ref), (1, nu_ref)):
        w_s[m, 160:HID, :] = jnp.zeros((HID - 160, 2048), BF)
        w_s[m, NEW_AT : NEW_AT + NEW, :] = new[...]
    down_ref[160:HID, :] = jnp.zeros((HID - 160, 2048), BF)
    down_ref[NEW_AT : NEW_AT + NEW, :] = nd_ref[...]
    for first, half in ((2, zh), (6, 1 - zh)):
        for k in range(NX):
            ref = get(first + k)
            source = half * NX + ((at_x + NX - k) & (NX - 1))
            lanes = pl.ds(pl.multiple_of(source * 256, 256), 256)
            w_s[0, 0:DENSE, lanes] = ref[0]
            w_s[1, 0:DENSE, lanes] = ref[1]
            down_ref[0:DENSE, lanes] = ref[2]
    put(5)
    gu = lax.dot_general(
        w_s[...].reshape(2 * HID, 2048), in_ref[...], NT, preferred_element_type=F32
    )
    gu_ref[...] = gu
    put(3)
    gate, up = gu[0:HID], gu[HID : 2 * HID]
    hidden = gate * jax.nn.sigmoid(gate) * up
    hid_ref[...] = hidden.astype(BF)
    put(4)
    rows = hidden.T.astype(BF)
    for y in range(NY):
        d = lax.dot_general(
            down_ref[:, y * 512 : (y + 1) * 512], perm, NT, preferred_element_type=F32
        ).astype(BF)
        o = jnp.dot(rows, d, preferred_element_type=F32)
        for x in range(NX):
            part_ref[x * NY + y] = o[x * ROWS : (x + 1) * ROWS, 0:256]
            away_ref[x * NY + y] = o[x * ROWS : (x + 1) * ROWS, 256:512].astype(BF)
    put(1)
    put(0)


def grad_kernel(at_ref, get, outs, put, sg_s):
    join(get(0), get(1), spread(at_ref[1]), sg_s)
    in_ref, gu_ref, hid_ref, down_ref = get(2), get(3), get(4), get(5)
    sg = sg_s[...]
    inp = in_ref[...]
    gate, up = gu_ref[0:HID], gu_ref[HID : 2 * HID]
    sig = jax.nn.sigmoid(gate)
    gh = lax.dot_general(down_ref[...], sg, NT, preferred_element_type=F32)
    ggp = (gh * up * sig * (1.0 + gate * (1.0 - sig))).astype(BF)
    gup = (gh * (gate * sig)).astype(BF)
    for i, (lhs, rhs) in enumerate(((hid_ref[...], sg), (ggp, inp), (gup, inp))):
        out = outs[i]
        g = jnp.dot(lhs, rhs, preferred_element_type=F32).astype(BF)
        out[0:DENSE, :] = g[0:DENSE]
        out[DENSE : DENSE + NEW, :] = g[NEW_AT : NEW_AT + NEW]
        put(i)


def combine_kernel(at, get, outs, put):
    (send_ref,) = outs
    r_ref, back_ref, ws_ref = get(0), get(1), get(2)
    sums = []
    for x in range(NX):
        s = r_ref[x * NY].astype(F32)
        for y in range(1, NY):
            s = s + r_ref[x * NY + y].astype(F32)
        sums.append(s)
    for b in range(ZH):
        s = jnp.concatenate([v[b * CAP : (b + 1) * CAP] for v in sums], axis=0)
        s = s * ws_ref[b, :, 0:1]
        hi = s.astype(BF)
        lo = (s - hi.astype(F32)).astype(BF)
        m = jnp.dot(back_ref[b], hi, preferred_element_type=F32) + jnp.dot(
            back_ref[b], lo, preferred_element_type=F32
        )
        send_ref[b * ZL : (b + 1) * ZL] = m.T.astype(BF).reshape(ZL, 32, 128)
    put(0)


def swap(v, axis):
    return lax.ppermute(v, axis, [(0, 1), (1, 0)])


def turn(v, k):
    return lax.ppermute(v, "x", [(i, (i + k) % NX) for i in range(NX)])


def exchange(v, axes):
    return lax.all_to_all(v, axes, 0, 0, tiled=True)


def local(
    tokens,
    cotangent,
    expert_ids,
    route_weights,
    dense_gate,
    dense_up,
    dense_down,
    noise_gate,
    noise_up,
    noise_down,
):
    Z, XY = ("zh", "zl"), ("x", "y")
    at = jnp.stack([lax.axis_index(n) for n in ("zh", "c", "x")]).astype(jnp.int32)
    hid = dense_down.shape[0] + noise_down.shape[1]

    mine = jnp.stack([dense_gate.T, dense_up.T, dense_down])
    theirs = swap(mine, "zh")
    (payload,) = call(
        pack_kernel,
        [sds((16, 72, 128), BF)],
        [expert_ids.T, route_weights.T, tokens.T, cotangent.T],
    )
    near = [mine] + [turn(mine, k) for k in range(1, NX)]
    got = exchange(payload, Z)
    got, theirs = lax.optimization_barrier((got, theirs))
    tok_send, cot_send, back, ws = call(
        select_kernel,
        [
            sds((16, ROWS, 256), BF),
            sds((16, ROWS, 256), BF),
            sds((ZH, 128, NX * CAP), BF),
            sds((ZH, NX * CAP, 128), F32),
        ],
        [got],
        scalars=at,
        direct=0,
    )
    tok_send, near = lax.optimization_barrier((tok_send, near))
    own = exchange(tok_send, XY)
    two, one, three = turn(theirs, 2), turn(theirs, 1), turn(theirs, 3)
    far = [theirs, one, two, three]
    oth = swap(own, "c")
    own, two, one, three = lax.optimization_barrier((own, two, one, three))
    far = [theirs, one, two, three]
    oth = swap(own, "c")
    cot_send, _ = lax.optimization_barrier((cot_send, own))
    own_cot = exchange(cot_send, XY)
    oth_cot = swap(own_cot, "c")

    part, away, inp, gu, hidden, down = call(
        forward_kernel,
        [
            sds((16, ROWS, 256), F32),
            sds((16, ROWS, 256), BF),
            sds((NX * ROWS, 2048), BF),
            sds((2 * HID, NX * ROWS), F32),
            sds((HID, NX * ROWS), BF),
            sds((HID, 2048), BF),
        ],
        [own, oth, *near, *far, noise_gate[0].T, noise_up[0].T, noise_down[0]],
        [pltpu.VMEM((2, HID, 2048), BF)],
        mib=32,
        scalars=at,
        direct=1,
    )
    send = (part + swap(away, "c").astype(F32)).astype(BF)
    own_cot, oth_cot, send = lax.optimization_barrier((own_cot, oth_cot, send))
    gd, gg, gup = call(
        grad_kernel,
        [sds((hid, 2048), BF)] * 3,
        [own_cot, oth_cot, inp, gu, hidden, down],
        [pltpu.VMEM((NX * ROWS, 2048), BF)],
        mib=32,
        scalars=at,
    )
    got = exchange(send, XY)
    (send,) = call(combine_kernel, [sds((16, 32, 128), BF)], [got, back, ws], direct=0)
    got = exchange(send, Z)
    mixed = jnp.sum(got.astype(F32), axis=0).astype(BF).T
    return mixed, gg[None], gup[None], gd[None]


def solution(mesh):
    e, s = ("zh", "x"), ("y", "zl", "c")
    fine = Mesh(mesh.devices.reshape(ZH, NX, NY, ZL, NC), e + s)
    in_specs = (
        P(e, s),
        P(e, s),
        P(e, None),
        P(e, None),
        P(e, s),
        P(e, s),
        P(s, e),
        P(e, None, s),
        P(e, None, s),
        P(e, s, None),
    )
    out_specs = (P(e, s), P(e, s, None), P(e, s, None), P(e, s, None))
    return jax.shard_map(local, mesh=fine, in_specs=in_specs, out_specs=out_specs, check_vma=False)
```

```python
import jax
import jax.numpy as jnp
from jax import lax
from jax.experimental import pallas as pl
from jax.experimental.pallas import tpu as pltpu
from jax.sharding import Mesh, PartitionSpec as P

BF = jnp.bfloat16
F32 = jnp.float32
ZH, NX, NY, ZL, NC = 2, 4, 4, 8, 2
CAP = 48
ROWS = 2 * CAP
NT = (((1,), (1,)), ((), ()))
VM = pl.BlockSpec(memory_space=pltpu.VMEM)
HB = pl.BlockSpec(memory_space=pltpu.HBM)
SM = pl.BlockSpec(memory_space=pltpu.SMEM)


def call(body, out_shape, operands, scratch=(), mib=8, scalars=None, direct=None):
    n, m = len(operands), len(out_shape)

    def kernel(*refs):
        refs = list(refs)
        at = refs.pop(0) if scalars is not None else None
        ins, outs, rest = refs[:n], refs[n : n + m], refs[n + m :]
        in_bufs, out_bufs, rest = rest[:n], rest[n : n + m], rest[n + m :]
        in_sem, out_sem, rest = rest[0], rest[1], rest[2:]
        copies = {
            i: pltpu.make_async_copy(ins[i], in_bufs[i], in_sem.at[i])
            for i in range(n)
            if i != direct
        }
        for copy in copies.values():
            copy.start()

        def get(i):
            if i == direct:
                return ins[i]
            copies[i].wait()
            return in_bufs[i]

        written = []

        def put(i):
            copy = pltpu.make_async_copy(out_bufs[i], outs[i], out_sem.at[i])
            copy.start()
            written.append(copy)

        body(at, get, out_bufs, put, *rest)
        for copy in written:
            copy.wait()

    return pl.pallas_call(
        kernel,
        out_shape=tuple(pltpu.HBM(o.shape, o.dtype) for o in out_shape),
        in_specs=([SM] if scalars is not None else [])
        + [VM if i == direct else HB for i in range(n)],
        out_specs=(HB,) * m,
        scratch_shapes=[
            pltpu.VMEM((8, 128) if i == direct else o.shape, o.dtype)
            for i, o in enumerate(operands)
        ]
        + [pltpu.VMEM(o.shape, o.dtype) for o in out_shape]
        + [pltpu.SemaphoreType.DMA((n,)), pltpu.SemaphoreType.DMA((m,))]
        + list(scratch),
        compiler_params=pltpu.CompilerParams(vmem_limit_bytes=mib * 1024 * 1024),
    )(
        *(() if scalars is None else (scalars,)),
        *[
            o if i == direct else pltpu.with_memory_space_constraint(o, pltpu.HBM)
            for i, o in enumerate(operands)
        ],
    )


def sds(shape, dtype):
    return jax.ShapeDtypeStruct(shape, dtype)


def pack_kernel(at, get, outs, put):
    (a_ref,) = outs
    id_ref, w_ref, tok_ref, cot_ref = get(0), get(1), get(2), get(3)
    w = w_ref[...]
    high = w.astype(BF).astype(F32)
    mid = (w - high).astype(BF).astype(F32)
    low = w - high - mid
    meta = jnp.concatenate([id_ref[...].astype(F32), high, mid, low], axis=0).astype(BF)
    a_ref[0:32, :] = tok_ref[...]
    a_ref[32:64, :] = cot_ref[...]
    a_ref[64:72, :] = meta
    put(0)


def select_kernel(at_ref, get, outs, put):
    tok_ref, cot_ref, back_ref, ws_ref = outs
    r_ref = get(0)
    zh = at_ref[0]
    row8 = lax.broadcasted_iota(jnp.int32, (8, 128), 0)
    expert = jnp.where(row8 < NX, zh * NX + row8, -1).astype(F32)
    before = (
        lax.broadcasted_iota(jnp.int32, (128, 128), 0)
        < lax.broadcasted_iota(jnp.int32, (128, 128), 1)
    ).astype(F32).astype(BF)
    slot = lax.broadcasted_iota(jnp.int32, (CAP, 128), 0).astype(F32)
    for b in range(ZH):
        meta = r_ref[b * ZL, 64:72, :].astype(F32)
        id0, id1 = meta[0:1], meta[1:2]
        w0 = meta[2:3] + meta[4:5] + meta[6:7]
        w1 = meta[3:4] + meta[5:6] + meta[7:8]
        is0 = expert == id0
        is1 = expert == id1
        member = jnp.where(is0 | is1, 1.0, 0.0)
        weight = jnp.where(is0, w0, jnp.where(is1, w1, 0.0))
        earlier = jnp.dot(member.astype(BF), before, preferred_element_type=F32)
        hits, ws = [], []
        for x in range(NX):
            hit = jnp.where(
                (member[x : x + 1] > 0.5) & (earlier[x : x + 1] == slot), 1.0, 0.0
            )
            hits.append(hit)
            ws.append(jnp.sum(hit * weight[x : x + 1], axis=1, keepdims=True))
        hit = jnp.concatenate(hits, axis=0)
        wslot = jnp.concatenate(ws, axis=0)
        one = hit.astype(BF)
        back_ref[b] = hit.T.astype(BF)
        ws_ref[b] = jnp.broadcast_to(wslot, (NX * CAP, 128))
        for at, scale, dst in ((0, None, tok_ref), (32, wslot, cot_ref)):
            v = r_ref[b * ZL : (b + 1) * ZL, at : at + 32, :].reshape(ZL * 32, 128)
            v = lax.dot_general(one, v, NT, preferred_element_type=F32)
            v = (v if scale is None else v * scale).astype(BF)
            for x in range(NX):
                for y in range(NY):
                    dst[x * NY + y, b * CAP : (b + 1) * CAP, :] = v[x * CAP : (x + 1) * CAP]
    for i in range(4):
        put(i)


def spread(c):
    j = lax.broadcasted_iota(jnp.int32, (512, 512), 0)
    f = lax.broadcasted_iota(jnp.int32, (512, 512), 1)
    src = jnp.where(((f >> 5) & 1) == c, 0, 256) + ((f >> 6) << 5) + (f & 31)
    return jnp.where(j == src, 1.0, 0.0).astype(BF)


def join(own_ref, oth_ref, perm, dst):
    for y in range(NY):
        rows = jnp.concatenate(
            [
                jnp.concatenate([own_ref[x * NY + y], oth_ref[x * NY + y]], axis=1)
                for x in range(NX)
            ],
            axis=0,
        )
        dst[:, y * 512 : (y + 1) * 512] = jnp.dot(
            rows, perm, preferred_element_type=F32
        ).astype(BF)


HID = 208
DENSE, NEW_AT, NEW = 172, 176, 20


def forward_kernel(at_ref, get, outs, put, w_s):
    part_ref, away_ref, in_ref, gu_ref, hid_ref, down_ref = outs
    zh, c, at_x = at_ref[0], at_ref[1], at_ref[2]
    perm = spread(c)
    join(get(0), get(1), perm, in_ref)
    put(2)
    ng_ref, nu_ref, nd_ref = get(10), get(11), get(12)
    for m, new in ((0, ng_ref), (1, nu_ref)):
        w_s[m, 160:HID, :] = jnp.zeros((HID - 160, 2048), BF)
        w_s[m, NEW_AT : NEW_AT + NEW, :] = new[...]
    down_ref[160:HID, :] = jnp.zeros((HID - 160, 2048), BF)
    down_ref[NEW_AT : NEW_AT + NEW, :] = nd_ref[...]
    for first, half in ((2, zh), (6, 1 - zh)):
        for k in range(NX):
            ref = get(first + k)
            source = half * NX + ((at_x + NX - k) & (NX - 1))
            lanes = pl.ds(pl.multiple_of(source * 256, 256), 256)
            w_s[0, 0:DENSE, lanes] = ref[0]
            w_s[1, 0:DENSE, lanes] = ref[1]
            down_ref[0:DENSE, lanes] = ref[2]
    put(5)
    gu = lax.dot_general(
        w_s[...].reshape(2 * HID, 2048), in_ref[...], NT, preferred_element_type=F32
    )
    gu_ref[...] = gu
    put(3)
    gate, up = gu[0:HID], gu[HID : 2 * HID]
    hidden = gate * jax.nn.sigmoid(gate) * up
    hid_ref[...] = hidden.astype(BF)
    put(4)
    rows = hidden.T.astype(BF)
    for y in range(NY):
        d = lax.dot_general(
            down_ref[:, y * 512 : (y + 1) * 512], perm, NT, preferred_element_type=F32
        ).astype(BF)
        o = jnp.dot(rows, d, preferred_element_type=F32)
        for x in range(NX):
            part_ref[x * NY + y] = o[x * ROWS : (x + 1) * ROWS, 0:256]
            away_ref[x * NY + y] = o[x * ROWS : (x + 1) * ROWS, 256:512].astype(BF)
    put(1)
    put(0)


def grad_kernel(at_ref, get, outs, put, sg_s):
    join(get(0), get(1), spread(at_ref[1]), sg_s)
    in_ref, gu_ref, hid_ref, down_ref = get(2), get(3), get(4), get(5)
    sg = sg_s[...]
    inp = in_ref[...]
    gate, up = gu_ref[0:HID], gu_ref[HID : 2 * HID]
    sig = jax.nn.sigmoid(gate)
    gh = lax.dot_general(down_ref[...], sg, NT, preferred_element_type=F32)
    ggp = (gh * up * sig * (1.0 + gate * (1.0 - sig))).astype(BF)
    gup = (gh * (gate * sig)).astype(BF)
    for i, (lhs, rhs) in enumerate(((hid_ref[...], sg), (ggp, inp), (gup, inp))):
        out = outs[i]
        g = jnp.dot(lhs, rhs, preferred_element_type=F32).astype(BF)
        out[0:DENSE, :] = g[0:DENSE]
        out[DENSE : DENSE + NEW, :] = g[NEW_AT : NEW_AT + NEW]
        put(i)


def combine_kernel(at, get, outs, put):
    (send_ref,) = outs
    r_ref, back_ref, ws_ref = get(0), get(1), get(2)
    sums = []
    for x in range(NX):
        s = r_ref[x * NY].astype(F32)
        for y in range(1, NY):
            s = s + r_ref[x * NY + y].astype(F32)
        sums.append(s)
    for b in range(ZH):
        s = jnp.concatenate([v[b * CAP : (b + 1) * CAP] for v in sums], axis=0)
        s = s * ws_ref[b, :, 0:1]
        hi = s.astype(BF)
        lo = (s - hi.astype(F32)).astype(BF)
        m = jnp.dot(back_ref[b], hi, preferred_element_type=F32) + jnp.dot(
            back_ref[b], lo, preferred_element_type=F32
        )
        send_ref[b * ZL : (b + 1) * ZL] = m.T.astype(BF).reshape(ZL, 32, 128)
    put(0)


def swap(v, axis):
    return lax.ppermute(v, axis, [(0, 1), (1, 0)])


def turn(v, k):
    return lax.ppermute(v, "x", [(i, (i + k) % NX) for i in range(NX)])


def exchange(v, axes):
    return lax.all_to_all(v, axes, 0, 0, tiled=True)


def local(
    tokens,
    cotangent,
    expert_ids,
    route_weights,
    dense_gate,
    dense_up,
    dense_down,
    noise_gate,
    noise_up,
    noise_down,
):
    Z, XY = ("zh", "zl"), ("x", "y")
    at = jnp.stack([lax.axis_index(n) for n in ("zh", "c", "x")]).astype(jnp.int32)
    hid = dense_down.shape[0] + noise_down.shape[1]

    mine = jnp.stack([dense_gate.T, dense_up.T, dense_down])
    theirs = swap(mine, "zh")
    (payload,) = call(
        pack_kernel,
        [sds((72, 128), BF)],
        [expert_ids.T, route_weights.T, tokens.T, cotangent.T],
    )
    near = [mine] + [turn(mine, k) for k in range(1, NX)]
    got = lax.all_gather(payload, Z, axis=0, tiled=False)
    got, theirs = lax.optimization_barrier((got, theirs))
    tok_send, cot_send, back, ws = call(
        select_kernel,
        [
            sds((16, ROWS, 256), BF),
            sds((16, ROWS, 256), BF),
            sds((ZH, 128, NX * CAP), BF),
            sds((ZH, NX * CAP, 128), F32),
        ],
        [got],
        scalars=at,
        direct=0,
    )
    tok_send, near = lax.optimization_barrier((tok_send, near))
    own = exchange(tok_send, XY)
    two, one, three = turn(theirs, 2), turn(theirs, 1), turn(theirs, 3)
    far = [theirs, one, two, three]
    oth = swap(own, "c")
    own, two, one, three = lax.optimization_barrier((own, two, one, three))
    far = [theirs, one, two, three]
    oth = swap(own, "c")
    cot_send, _ = lax.optimization_barrier((cot_send, own))
    own_cot = exchange(cot_send, XY)
    oth_cot = swap(own_cot, "c")

    part, away, inp, gu, hidden, down = call(
        forward_kernel,
        [
            sds((16, ROWS, 256), F32),
            sds((16, ROWS, 256), BF),
            sds((NX * ROWS, 2048), BF),
            sds((2 * HID, NX * ROWS), F32),
            sds((HID, NX * ROWS), BF),
            sds((HID, 2048), BF),
        ],
        [own, oth, *near, *far, noise_gate[0].T, noise_up[0].T, noise_down[0]],
        [pltpu.VMEM((2, HID, 2048), BF)],
        mib=32,
        scalars=at,
        direct=1,
    )
    send = (part + swap(away, "c").astype(F32)).astype(BF)
    own_cot, oth_cot, send = lax.optimization_barrier((own_cot, oth_cot, send))
    gd, gg, gup = call(
        grad_kernel,
        [sds((hid, 2048), BF)] * 3,
        [own_cot, oth_cot, inp, gu, hidden, down],
        [pltpu.VMEM((NX * ROWS, 2048), BF)],
        mib=32,
        scalars=at,
    )
    got = exchange(send, XY)
    (send,) = call(combine_kernel, [sds((16, 32, 128), BF)], [got, back, ws], direct=0)
    got = exchange(send, Z)
    mixed = jnp.sum(got.astype(F32), axis=0).astype(BF).T
    return mixed, gg[None], gup[None], gd[None]


def solution(mesh):
    e, s = ("zh", "x"), ("y", "zl", "c")
    fine = Mesh(mesh.devices.reshape(ZH, NX, NY, ZL, NC), e + s)
    in_specs = (
        P(e, s),
        P(e, s),
        P(e, None),
        P(e, None),
        P(e, s),
        P(e, s),
        P(s, e),
        P(e, None, s),
        P(e, None, s),
        P(e, s, None),
    )
    out_specs = (P(e, s), P(e, s, None), P(e, s, None), P(e, s, None))
    return jax.shard_map(local, mesh=fine, in_specs=in_specs, out_specs=out_specs, check_vma=False)
```
